512 devices in a mesh: dp: 64 (over z, y_hi, core), shard: 8 (over y_lo, x).
Axes of the slice: x: 4, y: 8 (y_hi: 4, y_lo: 2; y = y_hi * 2 + y_lo), z: 8, core: 2. Of those that a mesh axis runs over, the one named last changes fastest.
Arguments:
- tokens: bfloat16 [1024, 6144], P('dp', 'shard'), may hold values from -6 to 6
- cotangent: bfloat16 [1024, 6144], P('dp', 'shard'), may hold values from -6 to 6
- slot_token: int32 [1, 256], replicated, may hold values from 0 to 1023, as said below
- slot_gate: float32 [1, 256], replicated, may hold values from 0.1 to 0.9
- w_gate: bfloat16 [1, 6144, 16384], P(None, 'shard', 'dp'), may hold values from -0.078125 to 0.078125
- w_up: bfloat16 [1, 6144, 16384], P(None, 'shard', 'dp'), may hold values from -0.078125 to 0.078125
- w_down: bfloat16 [1, 16384, 6144], P(None, 'dp', 'shard'), may hold values from -0.046875 to 0.046875
Outputs:
- mixed: bfloat16 [1024, 6144], P('dp', 'shard')
- grad_tokens: bfloat16 [1024, 6144], P('dp', 'shard')
- grad_gate: bfloat16 [1, 6144, 16384], P(None, 'shard', 'dp')
- grad_up: bfloat16 [1, 6144, 16384], P(None, 'shard', 'dp')
- grad_down: bfloat16 [1, 16384, 6144], P(None, 'dp', 'shard')
The draws below stay inside these ranges and needn't reach their ends.
Inputs may be any that keep to these rules, and one draw needn't show every extreme that they name: `slot_token`: each row lists 256 distinct tokens; a token may sit in several rows.
All inputs are finite; a program needn't handle non-finite values.
Results may differ from the reference program's by a relative error of at most 0.006.
Values may be sent and summed in bfloat16 or wider, within the bound.
No kernel may reach another device: no remote copies, remote signals or barrier semaphores. Data moves between devices by JAX's collectives and lax.ppermute only.
A program may use at most 64 MiB of HBM per device.

```python
import jax
import jax.numpy as jnp

D = 6144
FF = 16384
E_WIN = 1
TOKENS = 1024
CAP = 256


def draw_slot_token(key, part):

    def expert_slots(subkey):
        first_key, second_key = jax.random.split(subkey)
        middle = jax.random.permutation(first_key, TOKENS - 2)[:CAP - 2].astype(jnp.int32) + 1
        picked = jnp.concatenate([jnp.zeros((1,), jnp.int32), middle, jnp.full((1,), TOKENS - 1, jnp.int32)])
        order = jax.random.permutation(second_key, CAP).astype(jnp.int32)
        return picked[order]
    subkeys = jax.random.split(jax.random.fold_in(key, 7), E_WIN)
    return jax.vmap(expert_slots)(subkeys)


def level_of(own_key, dims, cuts, low, top_value):
    factor_of, own = 1.0, jax.random.fold_in(own_key, 6)
    for axis_at, parts in cuts:
        steps = jnp.exp(jax.random.uniform(jax.random.fold_in(own, axis_at), (parts,), jnp.float32, low / len(cuts), top_value / len(cuts)))
        factor_of = factor_of * jnp.repeat(steps, dims[axis_at] // parts).reshape([-1 if axis == axis_at else 1 for axis in range(len(dims))])
    return factor_of


def bell_draw(own_key, dims, deviation, limit, cuts=(), dtype=jnp.bfloat16):
    loudness = level_of(own_key, dims, cuts, -0.22, 0.18) if cuts else 1.0
    drawn = jax.random.normal(own_key, dims, jnp.float32) * deviation * loudness
    return jnp.minimum(jnp.maximum(drawn, -limit), limit).astype(dtype)


def setup_inputs(seed: int = 0) -> dict:
    splits = jax.random.split(jax.random.key(seed), 8)
    tokens = bell_draw(splits[0], (TOKENS, D), 1.0, 6.0, ((0, 64), (1, 8)))
    cotangent = bell_draw(splits[1], (TOKENS, D), 1.0, 6.0, ((0, 64), (1, 8)))
    slot_token = draw_slot_token(jax.random.fold_in(splits[7], 71), 0)
    slot_gate = jnp.clip(jax.random.uniform(splits[3], (E_WIN, CAP), jnp.float32, 0.1, 0.9), 0.1, 0.9)
    w_gate = bell_draw(splits[4], (E_WIN, D, FF), D ** -0.5, 0.078125, ((1, 8), (2, 64)))
    w_up = bell_draw(splits[5], (E_WIN, D, FF), D ** -0.5, 0.078125, ((1, 8), (2, 64)))
    w_down = bell_draw(splits[6], (E_WIN, FF, D), FF ** -0.5, 0.046875, ((1, 64), (2, 8)))
    return dict(tokens=tokens, cotangent=cotangent, slot_token=slot_token, slot_gate=slot_gate, w_gate=w_gate, w_up=w_up, w_down=w_down)


def reference(tokens, cotangent, slot_token, slot_gate, w_gate, w_up, w_down):
    out_total = jnp.zeros((TOKENS, D), jnp.float32)
    back_total = jnp.zeros((TOKENS, D), jnp.float32)
    grads_gate = []
    grads_up = []
    grads_down = []
    for expert in range(E_WIN):
        picked = slot_token[expert].astype(jnp.int32)
        weight = slot_gate[expert].astype(jnp.float32)
        inputs = tokens[picked]
        gate_pre = jnp.dot(inputs, w_gate[expert], preferred_element_type=jnp.float32)
        up_pre = jnp.dot(inputs, w_up[expert], preferred_element_type=jnp.float32)
        sigmoid_gate = jax.nn.sigmoid(gate_pre)
        hidden = (gate_pre * sigmoid_gate * up_pre).astype(jnp.bfloat16)
        out_slots = jnp.dot(hidden, w_down[expert], preferred_element_type=jnp.float32).astype(jnp.bfloat16)
        out_total = out_total.at[picked].add(weight[:, None] * out_slots.astype(jnp.float32))
        scaled = (weight[:, None] * cotangent[picked].astype(jnp.float32)).astype(jnp.bfloat16)
        grads_down.append(jnp.dot(hidden.T, scaled, preferred_element_type=jnp.float32).astype(jnp.bfloat16))
        grad_hidden = jnp.dot(scaled, w_down[expert].T, preferred_element_type=jnp.float32)
        grad_gate_pre = (grad_hidden * up_pre * sigmoid_gate * (1.0 + gate_pre * (1.0 - sigmoid_gate))).astype(jnp.bfloat16)
        grad_up_pre = (grad_hidden * gate_pre * sigmoid_gate).astype(jnp.bfloat16)
        grads_gate.append(jnp.dot(inputs.T, grad_gate_pre, preferred_element_type=jnp.float32).astype(jnp.bfloat16))
        grads_up.append(jnp.dot(inputs.T, grad_up_pre, preferred_element_type=jnp.float32).astype(jnp.bfloat16))
        back_slots = (jnp.dot(grad_gate_pre, w_gate[expert].T, preferred_element_type=jnp.float32)
                      + jnp.dot(grad_up_pre, w_up[expert].T, preferred_element_type=jnp.float32)).astype(jnp.bfloat16)
        back_total = back_total.at[picked].add(back_slots.astype(jnp.float32))
    mixed = out_total.astype(jnp.bfloat16)
    grad_tokens = back_total.astype(jnp.bfloat16)
    return (mixed, grad_tokens, jnp.stack(grads_gate), jnp.stack(grads_up), jnp.stack(grads_down))
```

```python
import jax
import jax.numpy as jnp
from jax import lax
from jax.sharding import Mesh
from jax.sharding import PartitionSpec as P

BF16 = jnp.bfloat16
F32 = jnp.float32
CHIPS = ("z", "yh")
SHARD = ("yl", "x")
DP = ("z", "yh", "core")
SIZES = {"z": 8, "yh": 4, "core": 2, "yl": 2, "x": 4}


def exchange(rows, axes):
    n = lax.axis_size(axes)
    blocks = rows.reshape(n, rows.shape[0] // n, rows.shape[1])
    return lax.all_to_all(blocks, axes, 0, 0, tiled=True)


def spread(rows, axes):
    n = lax.axis_size(axes)
    blocks = jnp.broadcast_to(rows[None], (n, *rows.shape))
    out = lax.all_to_all(blocks, axes, 0, 0, tiled=True)
    return out.reshape(n * rows.shape[0], rows.shape[1])


def swap_core(rows):
    return lax.ppermute(rows, "core", [(0, 1), (1, 0)])


def dot(a, b, dims):
    return lax.dot_general(a, b, (dims, ((), ())), preferred_element_type=F32)


def on_device(tokens, cotangent, slot_token, slot_gate, w_gate, w_up, w_down):
    w_gate, w_up, w_down = w_gate[0], w_up[0], w_down[0]
    slots = slot_token.reshape(-1)
    gates = slot_gate.reshape(-1)
    n_slots = slots.shape[0]
    n_own = tokens.shape[0]
    chip = lax.axis_index(CHIPS)
    core = lax.axis_index("core")
    first = core == 0
    n_chips = lax.axis_size(CHIPS)

    keep = jnp.where(first, tokens, cotangent)
    recv = swap_core(jnp.where(first, cotangent, tokens))
    chip_rows = jnp.concatenate([keep, recv], axis=0)
    local = jnp.arange(n_own, dtype=jnp.int32)
    base = chip * (2 * n_own)
    own_ids = base + core * n_own + local
    other_ids = base + (1 - core) * n_own + local
    chip_ids = jnp.concatenate([own_ids, other_ids])
    pick = (slots[:, None] == chip_ids[None, :]).astype(BF16)

    sent = dot(pick, chip_rows, ((1,), (0,))).astype(BF16)
    mine = jnp.sum(exchange(sent, CHIPS).astype(F32), axis=0)
    per_chip = n_slots // n_chips
    my_gates = lax.dynamic_slice(gates, (chip * per_chip,), (per_chip,))[:, None]
    mine = jnp.where(first, mine, mine * my_gates).astype(BF16)
    rows = spread(mine, CHIPS)
    both = lax.all_gather(rows, "core", axis=0, tiled=False)
    inputs, scaled = both[0], both[1]

    parts = jnp.concatenate(
        [
            dot(inputs, w_gate, ((1,), (0,))).astype(BF16),
            dot(inputs, w_up, ((1,), (0,))).astype(BF16),
            dot(scaled, w_down, ((1,), (1,))).astype(BF16),
        ],
        axis=1,
    )
    sums = jnp.sum(exchange(parts, SHARD).astype(F32), axis=0)
    n_ff = w_gate.shape[1]
    gate_pre, up_pre, grad_hidden = sums[:, :n_ff], sums[:, n_ff : 2 * n_ff], sums[:, 2 * n_ff :]
    s = jax.nn.sigmoid(gate_pre)
    trio = jnp.concatenate(
        [
            (gate_pre * s * up_pre).astype(BF16),
            (grad_hidden * up_pre * s * (1.0 + gate_pre * (1.0 - s))).astype(BF16),
            (grad_hidden * gate_pre * s).astype(BF16),
        ],
        axis=1,
    )
    trio = spread(trio, SHARD)
    hidden, grad_gate_pre, grad_up_pre = trio[:, :n_ff], trio[:, n_ff : 2 * n_ff], trio[:, 2 * n_ff :]

    out_part = dot(hidden, w_down, ((1,), (0,)))
    back_part = dot(grad_gate_pre, w_gate, ((1,), (1,))) + dot(grad_up_pre, w_up, ((1,), (1,)))
    other = swap_core(jnp.where(first, back_part, out_part).astype(BF16))
    total = jnp.where(first, out_part, back_part) + other.astype(F32)
    slot_sum = jnp.sum(exchange(total.astype(BF16), CHIPS).astype(F32), axis=0).astype(BF16)
    slot_sum = jnp.where(first, (my_gates * slot_sum.astype(F32)).astype(BF16), slot_sum)
    slot_rows = spread(slot_sum, CHIPS)
    chip_out = dot(pick, slot_rows, ((0,), (0,))).astype(BF16)
    kept, handed = chip_out[:n_own], chip_out[n_own:]
    got = swap_core(handed)
    mixed = jnp.where(first, kept, got)
    grad_tokens = jnp.where(first, got, kept)

    grad_down = dot(hidden, scaled, ((0,), (0,))).astype(BF16)
    grad_gate = dot(inputs, grad_gate_pre, ((0,), (0,))).astype(BF16)
    grad_up = dot(inputs, grad_up_pre, ((0,), (0,))).astype(BF16)
    return (mixed, grad_tokens, grad_gate[None], grad_up[None], grad_down[None])


def solution(mesh):
    fine = Mesh(mesh.devices.reshape(tuple(SIZES.values())), tuple(SIZES))
    return jax.shard_map(
        on_device,
        mesh=fine,
        in_specs=(
            P(DP, SHARD),
            P(DP, SHARD),
            P(),
            P(),
            P(None, SHARD, DP),
            P(None, SHARD, DP),
            P(None, DP, SHARD),
        ),
        out_specs=(
            P(DP, SHARD),
            P(DP, SHARD),
            P(None, SHARD, DP),
            P(None, SHARD, DP),
            P(None, DP, SHARD),
        ),
        check_vma=False,
    )
```

```python
import jax
import jax.numpy as jnp
from jax import lax
from jax.sharding import Mesh
from jax.sharding import PartitionSpec as P

BF16 = jnp.bfloat16
F32 = jnp.float32
CHIPS = ("z", "yh")
SHARD = ("yl", "x")
DP = ("z", "yh", "core")
SIZES = {"z": 8, "yh": 4, "core": 2, "yl": 2, "x": 4}


def exchange(rows, axes):
    n = lax.axis_size(axes)
    blocks = rows.reshape(n, rows.shape[0] // n, rows.shape[1])
    return lax.all_to_all(blocks, axes, 0, 0, tiled=True)


def spread(rows, axes):
    n = lax.axis_size(axes)
    blocks = jnp.broadcast_to(rows[None], (n, *rows.shape))
    out = lax.all_to_all(blocks, axes, 0, 0, tiled=True)
    return out.reshape(n * rows.shape[0], rows.shape[1])


def swap_core(rows):
    return lax.ppermute(rows, "core", [(0, 1), (1, 0)])


def dot(a, b, dims):
    return lax.dot_general(a, b, (dims, ((), ())), preferred_element_type=F32)


def on_device(tokens, cotangent, slot_token, slot_gate, w_gate, w_up, w_down):
    w_gate, w_up, w_down = w_gate[0], w_up[0], w_down[0]
    slots = slot_token.reshape(-1)
    gates = slot_gate.reshape(-1)
    n_slots = slots.shape[0]
    n_own = tokens.shape[0]
    chip = lax.axis_index(CHIPS)
    core = lax.axis_index("core")
    first = core == 0
    n_chips = lax.axis_size(CHIPS)

    keep = jnp.where(first, tokens, cotangent)
    recv = swap_core(jnp.where(first, cotangent, tokens))
    chip_rows = jnp.concatenate([keep, recv], axis=0)
    local = jnp.arange(n_own, dtype=jnp.int32)
    base = chip * (2 * n_own)
    own_ids = base + core * n_own + local
    other_ids = base + (1 - core) * n_own + local
    chip_ids = jnp.concatenate([own_ids, other_ids])

    rank_here = jnp.sum((slots[:, None] < chip_ids[None, :]).astype(jnp.int32), axis=0)
    in_slot = jnp.max((slots[:, None] == chip_ids[None, :]).astype(jnp.int32), axis=0)
    peers = jnp.arange(n_chips, dtype=jnp.int32)
    lane = jnp.where(in_slot > 0, rank_here % n_chips, -1)
    pick = (peers[:, None] == lane[None, :]).astype(BF16)
    sent = dot(pick, chip_rows, ((1,), (0,))).astype(BF16)
    arrived = lax.all_to_all(sent, CHIPS, 0, 0, tiled=True)

    per_chip = n_slots // n_chips
    ranks = jnp.sum((slots[:, None] < slots[None, :]).astype(jnp.int32), axis=0)
    my_ranks = chip + n_chips * jnp.arange(per_chip, dtype=jnp.int32)
    match = ranks[None, :] == my_ranks[:, None]
    my_tokens = jnp.sum(jnp.where(match, slots[None, :], 0), axis=1)
    my_gates = jnp.sum(jnp.where(match, gates[None, :], 0.0), axis=1)[:, None]
    place = ((my_tokens // (2 * n_own))[:, None] == peers[None, :]).astype(BF16)
    mine = dot(place, arrived, ((1,), (0,)))
    mine = jnp.where(first, mine, mine * my_gates).astype(BF16)
    rows = spread(mine, CHIPS)
    both = lax.all_gather(rows, "core", axis=0, tiled=False)
    inputs, scaled = both[0], both[1]

    parts = jnp.concatenate(
        [
            dot(inputs, w_gate, ((1,), (0,))).astype(BF16),
            dot(inputs, w_up, ((1,), (0,))).astype(BF16),
            dot(scaled, w_down, ((1,), (1,))).astype(BF16),
        ],
        axis=1,
    )
    sums = jnp.sum(exchange(parts, SHARD).astype(F32), axis=0)
    n_ff = w_gate.shape[1]
    gate_pre, up_pre, grad_hidden = sums[:, :n_ff], sums[:, n_ff : 2 * n_ff], sums[:, 2 * n_ff :]
    s = jax.nn.sigmoid(gate_pre)
    trio = jnp.concatenate(
        [
            (gate_pre * s * up_pre).astype(BF16),
            (grad_hidden * up_pre * s * (1.0 + gate_pre * (1.0 - s))).astype(BF16),
            (grad_hidden * gate_pre * s).astype(BF16),
        ],
        axis=1,
    )
    trio = spread(trio, SHARD)
    hidden, grad_gate_pre, grad_up_pre = trio[:, :n_ff], trio[:, n_ff : 2 * n_ff], trio[:, 2 * n_ff :]

    out_part = dot(hidden, w_down, ((1,), (0,)))
    back_part = dot(grad_gate_pre, w_gate, ((1,), (1,))) + dot(grad_up_pre, w_up, ((1,), (1,)))
    other = swap_core(jnp.where(first, back_part, out_part).astype(BF16))
    total = jnp.where(first, out_part, back_part) + other.astype(F32)
    slot_sum = jnp.sum(exchange(total.astype(BF16), CHIPS).astype(F32), axis=0)
    slot_sum = lax.reduce_precision(slot_sum, 8, 7)
    slot_sum = jnp.where(first, my_gates * slot_sum, slot_sum).astype(BF16)
    back = dot(place, slot_sum, ((0,), (0,))).astype(BF16)
    returned = lax.all_to_all(back, CHIPS, 0, 0, tiled=True)
    chip_out = dot(pick, returned, ((0,), (0,))).astype(BF16)
    kept, handed = chip_out[:n_own], chip_out[n_own:]
    got = swap_core(handed)
    mixed = jnp.where(first, kept, got)
    grad_tokens = jnp.where(first, got, kept)

    grad_down = dot(hidden, scaled, ((0,), (0,))).astype(BF16)
    grad_gate = dot(inputs, grad_gate_pre, ((0,), (0,))).astype(BF16)
    grad_up = dot(inputs, grad_up_pre, ((0,), (0,))).astype(BF16)
    return (mixed, grad_tokens, grad_gate[None], grad_up[None], grad_down[None])


def solution(mesh):
    fine = Mesh(mesh.devices.reshape(tuple(SIZES.values())), tuple(SIZES))
    return jax.shard_map(
        on_device,
        mesh=fine,
        in_specs=(
            P(DP, SHARD),
            P(DP, SHARD),
            P(),
            P(),
            P(None, SHARD, DP),
            P(None, SHARD, DP),
            P(None, DP, SHARD),
        ),
        out_specs=(
            P(DP, SHARD),
            P(DP, SHARD),
            P(None, SHARD, DP),
            P(None, SHARD, DP),
            P(None, DP, SHARD),
        ),
        check_vma=False,
    )
```

```python
import jax
import jax.numpy as jnp
from jax import lax
from jax.experimental import pallas as pl
from jax.experimental.pallas import tpu as pltpu
from jax.sharding import Mesh
from jax.sharding import PartitionSpec as P

BF16 = jnp.bfloat16
F32 = jnp.float32
CHIPS = ("z", "yh")
SHARD = ("yl", "x")
DP = ("z", "yh", "core")
SIZES = {"z": 8, "yh": 4, "core": 2, "yl": 2, "x": 4}


def exchange(rows, axes):
    n = lax.axis_size(axes)
    blocks = rows.reshape(n, rows.shape[0] // n, rows.shape[1])
    return lax.all_to_all(blocks, axes, 0, 0, tiled=True)


def spread(rows, axes):
    n = lax.axis_size(axes)
    blocks = jnp.broadcast_to(rows[None], (n, *rows.shape))
    out = lax.all_to_all(blocks, axes, 0, 0, tiled=True)
    return out.reshape(n * rows.shape[0], rows.shape[1])


def from_cores(rows):
    return lax.all_gather(rows, "core", axis=0, tiled=False)


def dot(a, b, dims):
    return lax.dot_general(a, b, (dims, ((), ())), preferred_element_type=F32)


def on_vmem(kernel, shape, dtype, *operands):
    return pl.pallas_call(
        kernel,
        out_shape=jax.ShapeDtypeStruct(shape, dtype),
        in_specs=[pl.BlockSpec(memory_space=pltpu.VMEM)] * len(operands),
        out_specs=pl.BlockSpec(memory_space=pltpu.VMEM),
        compiler_params=pltpu.CompilerParams(vmem_limit_bytes=4 << 20),
    )(*operands)


LANES = 128
SEGMENTS = 8


def to_messages(rows, out_ref):
    used = rows.shape[1] // LANES
    for k in range(used):
        out_ref[:, k, :] = rows[:, k * LANES : (k + 1) * LANES]
    if used < SEGMENTS:
        out_ref[:, used:, :] = jnp.zeros((rows.shape[0], SEGMENTS - used, LANES), F32)


def from_messages(ref, used):
    return jnp.concatenate([ref[:, k, :] for k in range(used)], axis=1).astype(BF16)


def send_tokens(pick_ref, pairs_ref, out_ref):
    width = pairs_ref.shape[1] // 2
    first = lax.axis_index("core") == 0
    rows = jnp.where(first, pairs_ref[:, :width].astype(F32), pairs_ref[:, width:].astype(F32))
    to_messages(dot(pick_ref[...], rows.astype(BF16), ((1,), (0,))), out_ref)


def receive_tokens(place_ref, gates_ref, arrived_ref, out_ref):
    rows = from_messages(arrived_ref, out_ref.shape[2] // LANES)
    mine = dot(place_ref[...], rows, ((1,), (0,)))
    first = lax.axis_index("core") == 0
    mine = jnp.where(first, mine, mine * gates_ref[...]).astype(BF16)
    for q in range(out_ref.shape[0]):
        out_ref[q] = mine


def send_slots(place_t_ref, gates_ref, blocks_ref, out_ref):
    total = blocks_ref[0].astype(F32)
    for q in range(1, blocks_ref.shape[0]):
        total = total + blocks_ref[q].astype(F32)
    total = total.astype(BF16).astype(F32)
    first = lax.axis_index("core") == 0
    total = jnp.where(first, total * gates_ref[...], total).astype(BF16)
    to_messages(dot(place_t_ref[...], total, ((1,), (0,))), out_ref)


def receive_slots(pick_t_ref, arrived_ref, out_ref):
    rows = from_messages(arrived_ref, out_ref.shape[1] // LANES)
    out_ref[...] = dot(pick_t_ref[...], rows, ((1,), (0,))).astype(BF16)


def on_device(tokens, cotangent, slot_token, slot_gate, w_gate, w_up, w_down):
    w_gate, w_up, w_down = w_gate[0], w_up[0], w_down[0]
    slots = slot_token.reshape(-1)
    gates = slot_gate.reshape(-1)
    n_slots = slots.shape[0]
    n_own = tokens.shape[0]
    chip = lax.axis_index(CHIPS)
    core = lax.axis_index("core")
    first = core == 0
    n_chips = lax.axis_size(CHIPS)

    width = tokens.shape[1]
    pairs = from_cores(jnp.concatenate([tokens, cotangent], axis=1)).reshape(2 * n_own, -1)
    chip_ids = chip * (2 * n_own) + jnp.arange(2 * n_own, dtype=jnp.int32)

    joined = jnp.concatenate([w_gate.T, w_up.T, w_down], axis=0)
    n_ff = w_gate.shape[1]
    theirs = lax.ppermute(joined, "core", [(0, 1), (1, 0)])
    used = ((jnp.arange(3 * n_ff) >= 2 * n_ff) == first)[:, None]
    weights_0 = jnp.where(used, jnp.where(first, joined, theirs), jnp.zeros((), BF16))
    weights_1 = jnp.where(used, jnp.where(first, theirs, joined), jnp.zeros((), BF16))
    weights_0, weights_1 = lax.optimization_barrier((weights_0, weights_1))

    rank_here = jnp.sum((slots[:, None] < chip_ids[None, :]).astype(jnp.int32), axis=0)
    in_slot = jnp.max((slots[:, None] == chip_ids[None, :]).astype(jnp.int32), axis=0)
    peers = jnp.arange(n_chips, dtype=jnp.int32)
    lane = jnp.where(in_slot > 0, rank_here % n_chips, -1)
    pick = (peers[:, None] == lane[None, :]).astype(BF16)
    blocks = (n_chips, SEGMENTS, LANES)
    sent = on_vmem(send_tokens, blocks, F32, pick, pairs)
    arrived = lax.all_to_all(sent, CHIPS, 0, 0, tiled=True)

    per_chip = n_slots // n_chips
    ranks = jnp.sum((slots[:, None] < slots[None, :]).astype(jnp.int32), axis=0)
    my_ranks = chip + n_chips * jnp.arange(per_chip, dtype=jnp.int32)
    match = ranks[None, :] == my_ranks[:, None]
    my_tokens = jnp.sum(jnp.where(match, slots[None, :], 0), axis=1)
    my_gates = jnp.sum(jnp.where(match, gates[None, :], 0.0), axis=1)[:, None]
    place = ((my_tokens // (2 * n_own))[:, None] == peers[None, :]).astype(BF16)
    copies = on_vmem(receive_tokens, (n_chips, per_chip, width), BF16, place, my_gates, arrived)
    rows = lax.all_to_all(copies, CHIPS, 0, 0, tiled=True).reshape(n_slots, width)
    both = from_cores(rows)
    inputs, scaled = both[0], both[1]

    parts = jnp.concatenate(
        [
            dot(inputs, joined[: 2 * n_ff], ((1,), (1,))).astype(BF16),
            dot(scaled, w_down, ((1,), (1,))).astype(BF16),
        ],
        axis=1,
    )
    sums = jnp.sum(exchange(parts, SHARD).astype(F32), axis=0)
    gate_pre, up_pre, grad_hidden = sums[:, :n_ff], sums[:, n_ff : 2 * n_ff], sums[:, 2 * n_ff :]
    s = jax.nn.sigmoid(gate_pre)
    trio = jnp.concatenate(
        [
            (grad_hidden * up_pre * s * (1.0 + gate_pre * (1.0 - s))).astype(BF16),
            (grad_hidden * gate_pre * s).astype(BF16),
            (gate_pre * s * up_pre).astype(BF16),
        ],
        axis=1,
    )
    trio = spread(trio, SHARD)
    grad_gate_pre, grad_up_pre, hidden = trio[:, :n_ff], trio[:, n_ff : 2 * n_ff], trio[:, 2 * n_ff :]

    trios = from_cores(trio)
    total = dot(trios[0], weights_0, ((1,), (0,))) + dot(trios[1], weights_1, ((1,), (0,)))
    summands = exchange(total.astype(BF16), CHIPS)
    back = on_vmem(send_slots, blocks, F32, place.T, my_gates, summands)
    returned = lax.all_to_all(back, CHIPS, 0, 0, tiled=True)
    chip_out = on_vmem(receive_slots, (2 * n_own, width), BF16, pick.T, returned)
    done = from_cores(chip_out)
    mixed = lax.dynamic_slice_in_dim(done[0], core * n_own, n_own, 0)
    grad_tokens = lax.dynamic_slice_in_dim(done[1], core * n_own, n_own, 0)

    grad_down = dot(hidden, scaled, ((0,), (0,))).astype(BF16)
    grad_gate = dot(inputs, grad_gate_pre, ((0,), (0,))).astype(BF16)
    grad_up = dot(inputs, grad_up_pre, ((0,), (0,))).astype(BF16)
    return (mixed, grad_tokens, grad_gate[None], grad_up[None], grad_down[None])


def solution(mesh):
    fine = Mesh(mesh.devices.reshape(tuple(SIZES.values())), tuple(SIZES))
    return jax.shard_map(
        on_device,
        mesh=fine,
        in_specs=(
            P(DP, SHARD),
            P(DP, SHARD),
            P(),
            P(),
            P(None, SHARD, DP),
            P(None, SHARD, DP),
            P(None, DP, SHARD),
        ),
        out_specs=(
            P(DP, SHARD),
            P(DP, SHARD),
            P(None, SHARD, DP),
            P(None, SHARD, DP),
            P(None, DP, SHARD),
        ),
        check_vma=False,
    )
```

```python
import functools

import jax
import jax.numpy as jnp
from jax import lax
from jax.experimental import pallas as pl
from jax.experimental.pallas import tpu as pltpu
from jax.sharding import Mesh
from jax.sharding import PartitionSpec as P


BF16 = jnp.bfloat16
F32 = jnp.float32
CHIPS = ("z", "yh")
SHARD = ("yl", "x")
DP = ("z", "yh", "core")
SIZES = {"z": 8, "yh": 4, "core": 2, "yl": 2, "x": 4}


def exchange(rows, axes):
    n = lax.axis_size(axes)
    blocks = rows.reshape(n, rows.shape[0] // n, rows.shape[1])
    return lax.all_to_all(blocks, axes, 0, 0, tiled=True)


def spread(rows, axes):
    n = lax.axis_size(axes)
    blocks = jnp.broadcast_to(rows[None], (n, *rows.shape))
    out = lax.all_to_all(blocks, axes, 0, 0, tiled=True)
    return out.reshape(n * rows.shape[0], rows.shape[1])


def from_cores(rows):
    return lax.all_gather(rows, "core", axis=0, tiled=False)


def dot(a, b, dims):
    return lax.dot_general(a, b, (dims, ((), ())), preferred_element_type=F32)


def on_vmem(kernel, outs, *operands):
    vmem = pl.BlockSpec(memory_space=pltpu.VMEM)
    return pl.pallas_call(
        kernel,
        out_shape=tuple(jax.ShapeDtypeStruct(*o) for o in outs),
        in_specs=[vmem] * len(operands),
        out_specs=(vmem,) * len(outs),
        compiler_params=pltpu.CompilerParams(vmem_limit_bytes=4 << 20),
    )(*operands)


LANES = 128
SEGMENTS = 8


def to_messages(rows, out_ref):
    used = rows.shape[1] // LANES
    for k in range(used):
        out_ref[:, k, :] = rows[:, k * LANES : (k + 1) * LANES]
    if used < SEGMENTS:
        out_ref[:, used:, :] = jnp.zeros((rows.shape[0], SEGMENTS - used, LANES), F32)


def from_messages(ref, used):
    return jnp.concatenate([ref[:, k, :] for k in range(used)], axis=1).astype(BF16)


def send_tokens(slots_ref, pairs_ref, out_ref, pick_ref):
    n_tok, n_chips = pick_ref.shape
    n_slots = slots_ref.shape[1]
    chip = lax.axis_index("z") * lax.axis_size("yh") + lax.axis_index("yh")
    slots = slots_ref[...]

    ids = chip * n_tok + lax.broadcasted_iota(jnp.int32, (n_tok, n_slots), 0)
    row = jnp.broadcast_to(slots, (n_tok, n_slots))
    rank = jnp.sum(jnp.where(row < ids, 1.0, 0.0), axis=1, keepdims=True).astype(jnp.int32)
    held = jnp.sum(jnp.where(row == ids, 1.0, 0.0), axis=1, keepdims=True)
    peer = lax.broadcasted_iota(jnp.int32, (n_tok, n_chips), 1)
    lane = jnp.where(held > 0.0, lax.rem(rank, n_chips), -1)
    pick_ref[...] = jnp.where(peer == lane, 1.0, 0.0).astype(BF16)

    width = pairs_ref.shape[1] // 2
    first = lax.axis_index("core") == 0
    rows = jnp.where(first, pairs_ref[:, :width].astype(F32), pairs_ref[:, width:].astype(F32))
    to_messages(dot(pick_ref[...], rows.astype(BF16), ((0,), (0,))), out_ref)


def find_slots(n_tok, slots_ref, gates_ref, place_ref, my_gates_ref):
    per_chip, n_chips = place_ref.shape
    n_slots = slots_ref.shape[1]
    chip = lax.axis_index("z") * lax.axis_size("yh") + lax.axis_index("yh")
    slots = slots_ref[...]
    wide = jnp.broadcast_to(slots.astype(F32), (LANES, n_slots))
    column = jnp.transpose(wide)[:, :1]
    below = jnp.where(column < slots.astype(F32), 1.0, 0.0)
    ranks = jnp.sum(below, axis=0, keepdims=True).astype(jnp.int32)
    mine = chip + n_chips * lax.broadcasted_iota(jnp.int32, (per_chip, n_slots), 0)
    match = jnp.broadcast_to(ranks, (per_chip, n_slots)) == mine
    token = jnp.sum(jnp.where(match, slots.astype(F32), 0.0), axis=1, keepdims=True).astype(jnp.int32)
    my_gates_ref[...] = jnp.sum(jnp.where(match, gates_ref[...], 0.0), axis=1, keepdims=True)
    source = lax.broadcasted_iota(jnp.int32, (per_chip, n_chips), 1)
    place_ref[...] = jnp.where(lax.div(token, n_tok) == source, 1.0, 0.0).astype(BF16)


def receive_tokens(place_ref, gates_ref, arrived_ref, out_ref):
    rows = from_messages(arrived_ref, out_ref.shape[2] // LANES)
    mine = dot(place_ref[...], rows, ((1,), (0,)))
    first = lax.axis_index("core") == 0
    mine = jnp.where(first, mine, mine * gates_ref[...]).astype(BF16)
    for q in range(out_ref.shape[0]):
        out_ref[q] = mine


def send_slots(place_ref, gates_ref, blocks_ref, out_ref):
    total = blocks_ref[0].astype(F32)
    for q in range(1, blocks_ref.shape[0]):
        total = total + blocks_ref[q].astype(F32)
    total = total.astype(BF16).astype(F32)
    first = lax.axis_index("core") == 0
    total = jnp.where(first, total, total * gates_ref[...]).astype(BF16)
    to_messages(dot(place_ref[...], total, ((0,), (0,))), out_ref)


def receive_slots(pick_ref, arrived_ref, out_ref):
    rows = from_messages(arrived_ref, out_ref.shape[1] // LANES)
    out_ref[...] = dot(pick_ref[...], rows, ((1,), (0,))).astype(BF16)


def on_device(tokens, cotangent, slot_token, slot_gate, w_gate, w_up, w_down):
    w_gate, w_up, w_down = w_gate[0], w_up[0], w_down[0]
    n_ff = w_gate.shape[1]
    n_own, width = tokens.shape
    n_slots = slot_token.size
    core = lax.axis_index("core")
    first = core == 0
    n_chips = lax.axis_size(CHIPS)
    per_chip = n_slots // n_chips
    blocks = (n_chips, SEGMENTS, LANES)

    pairs = from_cores(jnp.concatenate([tokens, cotangent], axis=1)).reshape(2 * n_own, 2 * width)
    slots = slot_token.reshape(1, -1)
    sent, pick = on_vmem(send_tokens, ((blocks, F32), ((2 * n_own, n_chips), BF16)), slots, pairs)
    arrived = lax.all_to_all(sent, CHIPS, 0, 0, tiled=True)
    place, my_gates = on_vmem(
        functools.partial(find_slots, 2 * n_own),
        (((per_chip, n_chips), BF16), ((per_chip, 1), F32)),
        slots,
        slot_gate.reshape(1, -1),
    )
    gate_up = jnp.concatenate([w_gate.T, w_up.T], axis=0)
    blank = jnp.zeros_like(w_down)
    theirs = jnp.where(first, jnp.concatenate([w_down, blank], axis=0), gate_up)
    theirs = lax.ppermute(theirs, "core", [(0, 1), (1, 0)])
    weights = jnp.where(
        first,
        jnp.concatenate([gate_up, theirs], axis=0),
        jnp.concatenate([theirs[:n_ff], w_down, blank, blank], axis=0),
    )
    (copies,) = on_vmem(receive_tokens, (((n_chips, per_chip, width), BF16),), place, my_gates, arrived)
    rows = lax.all_to_all(copies, CHIPS, 0, 0, tiled=True).reshape(n_slots, width)
    weights, rows = lax.optimization_barrier((weights, rows))

    parts = dot(rows, weights, ((1,), (1,))).astype(BF16)
    sums = jnp.sum(exchange(parts, SHARD).astype(F32), axis=0)
    sums = from_cores(sums)
    trios = []
    for k in range(2):
        gate_pre = sums[0, :, 2 * k * n_ff : (2 * k + 1) * n_ff]
        up_pre = sums[0, :, (2 * k + 1) * n_ff : (2 * k + 2) * n_ff]
        grad_hidden = sums[1, :, k * n_ff : (k + 1) * n_ff]
        s = jax.nn.sigmoid(gate_pre)
        trios.append(
            (
                (gate_pre * s * up_pre).astype(BF16),
                (grad_hidden * up_pre * s * (1.0 + gate_pre * (1.0 - s))).astype(BF16),
                (grad_hidden * gate_pre * s).astype(BF16),
            )
        )
    (h0, g0, u0), (h1, g1, u1) = trios
    factors = jnp.concatenate(
        [jnp.where(first, g0, h0), jnp.where(first, u0, h1), g1, u1, jnp.where(first, h0, h1)], axis=1
    )
    factors = spread(factors, SHARD)

    total = dot(factors[:, : 4 * n_ff], weights, ((1,), (0,))).astype(BF16)
    total, rows = lax.optimization_barrier((total, rows))
    summands = exchange(total, CHIPS)
    other_rows = lax.ppermute(rows, "core", [(0, 1), (1, 0)])
    factors, rows, other_rows, summands = lax.optimization_barrier((factors, rows, other_rows, summands))
    (back,) = on_vmem(send_slots, ((blocks, F32),), place, my_gates, summands)
    returned = lax.all_to_all(back, CHIPS, 0, 0, tiled=True)
    (chip_out,) = on_vmem(receive_slots, (((2 * n_own, width), BF16),), pick, returned)
    done = from_cores(chip_out)
    grad_tokens = lax.dynamic_slice_in_dim(done[0], core * n_own, n_own, 0)
    mixed = lax.dynamic_slice_in_dim(done[1], core * n_own, n_own, 0)

    inputs = jnp.where(first, rows, other_rows)
    scaled = jnp.where(first, other_rows, rows)
    hidden = factors[:, 4 * n_ff :]
    grad_pre = lax.dynamic_slice_in_dim(factors, core * 2 * n_ff, 2 * n_ff, 1)
    grad_down = dot(hidden, scaled, ((0,), (0,))).astype(BF16)
    grad_gate = dot(inputs, grad_pre[:, :n_ff], ((0,), (0,))).astype(BF16)
    grad_up = dot(inputs, grad_pre[:, n_ff:], ((0,), (0,))).astype(BF16)
    return (mixed, grad_tokens, grad_gate[None], grad_up[None], grad_down[None])


def solution(mesh):
    fine = Mesh(mesh.devices.reshape(tuple(SIZES.values())), tuple(SIZES))
    return jax.shard_map(
        on_device,
        mesh=fine,
        in_specs=(
            P(DP, SHARD),
            P(DP, SHARD),
            P(),
            P(),
            P(None, SHARD, DP),
            P(None, SHARD, DP),
            P(None, DP, SHARD),
        ),
        out_specs=(
            P(DP, SHARD),
            P(DP, SHARD),
            P(None, SHARD, DP),
            P(None, SHARD, DP),
            P(None, DP, SHARD),
        ),
        check_vma=False,
    )
```

```python
import functools

import jax
import jax.numpy as jnp
from jax import lax
from jax.experimental import pallas as pl
from jax.experimental.pallas import tpu as pltpu
from jax.sharding import Mesh
from jax.sharding import PartitionSpec as P


BF16 = jnp.bfloat16
F32 = jnp.float32
CHIPS = ("z", "yh")
SHARD = ("yl", "x")
DP = ("z", "yh", "core")
SIZES = {"z": 8, "yh": 4, "core": 2, "yl": 2, "x": 4}


def exchange(rows, axes):
    n = lax.axis_size(axes)
    blocks = rows.reshape(n, rows.shape[0] // n, rows.shape[1])
    return lax.all_to_all(blocks, axes, 0, 0, tiled=True)


def spread(rows, axes):
    n = lax.axis_size(axes)
    blocks = jnp.broadcast_to(rows[None], (n, *rows.shape))
    out = lax.all_to_all(blocks, axes, 0, 0, tiled=True)
    return out.reshape(n * rows.shape[0], rows.shape[1])


def from_cores(rows):
    return lax.all_gather(rows, "core", axis=0, tiled=False)


def dot(a, b, dims):
    return lax.dot_general(a, b, (dims, ((), ())), preferred_element_type=F32)


def on_vmem(kernel, outs, *operands):
    vmem = pl.BlockSpec(memory_space=pltpu.VMEM)
    return pl.pallas_call(
        kernel,
        out_shape=tuple(jax.ShapeDtypeStruct(*o) for o in outs),
        in_specs=[vmem] * len(operands),
        out_specs=(vmem,) * len(outs),
        compiler_params=pltpu.CompilerParams(vmem_limit_bytes=4 << 20),
    )(*operands)


LANES = 128
ID_BASE = 32
SEGMENTS = 8


def to_messages(rows, out_ref):
    used = rows.shape[1] // LANES
    for k in range(used):
        out_ref[:, k, :] = rows[:, k * LANES : (k + 1) * LANES]
    if used < SEGMENTS:
        out_ref[:, used:, :] = jnp.zeros((rows.shape[0], SEGMENTS - used, LANES), F32)


def from_messages(ref, used):
    return jnp.concatenate([ref[:, k, :] for k in range(used)], axis=1).astype(BF16)


def send_tokens(n_slots, pairs_ref, out_ref, pick_ref):
    n_tok, n_chips = pick_ref.shape
    n_own = n_tok // 2
    width = pairs_ref.shape[2] // 2
    chip = lax.axis_index("z") * lax.axis_size("yh") + lax.axis_index("yh")
    parts = pairs_ref[0, n_own:, :n_slots].astype(F32)
    slots = parts[0:1] * float(ID_BASE) + parts[1:2]

    ids = (chip * n_tok + lax.broadcasted_iota(jnp.int32, (n_tok, n_slots), 0)).astype(F32)
    row = jnp.broadcast_to(slots, (n_tok, n_slots))
    rank = jnp.sum(jnp.where(row < ids, 1.0, 0.0), axis=1, keepdims=True).astype(jnp.int32)
    held = jnp.sum(jnp.where(row == ids, 1.0, 0.0), axis=1, keepdims=True)
    peer = lax.broadcasted_iota(jnp.int32, (n_tok, n_chips), 1)
    lane = jnp.where(held > 0.0, lax.rem(rank, n_chips), -1)
    pick_ref[...] = jnp.where(peer == lane, 1.0, 0.0).astype(BF16)

    first = lax.axis_index("core") == 0
    here = [
        jnp.where(first, pairs_ref[c, :n_own, :width].astype(F32), pairs_ref[c, :n_own, width:].astype(F32))
        for c in range(2)
    ]
    rows = jnp.concatenate(here, axis=0).astype(BF16)
    to_messages(dot(pick_ref[...], rows, ((0,), (0,))), out_ref)


def find_slots(n_tok, slots_ref, gates_ref, place_ref, my_gates_ref):
    per_chip, n_chips = place_ref.shape
    n_slots = slots_ref.shape[1]
    chip = lax.axis_index("z") * lax.axis_size("yh") + lax.axis_index("yh")
    slots = slots_ref[...]
    wide = jnp.broadcast_to(slots.astype(F32), (LANES, n_slots))
    column = jnp.transpose(wide)[:, :1]
    below = jnp.where(column < slots.astype(F32), 1.0, 0.0)
    ranks = jnp.sum(below, axis=0, keepdims=True).astype(jnp.int32)
    mine = chip + n_chips * lax.broadcasted_iota(jnp.int32, (per_chip, n_slots), 0)
    match = jnp.broadcast_to(ranks, (per_chip, n_slots)) == mine
    token = jnp.sum(jnp.where(match, slots.astype(F32), 0.0), axis=1, keepdims=True).astype(jnp.int32)
    my_gates_ref[...] = jnp.sum(jnp.where(match, gates_ref[...], 0.0), axis=1, keepdims=True)
    source = lax.broadcasted_iota(jnp.int32, (per_chip, n_chips), 1)
    place_ref[...] = jnp.where(lax.div(token, n_tok) == source, 1.0, 0.0).astype(BF16)


def receive_tokens(place_ref, gates_ref, arrived_ref, out_ref):
    rows = from_messages(arrived_ref, out_ref.shape[2] // LANES)
    mine = dot(place_ref[...], rows, ((1,), (0,)))
    first = lax.axis_index("core") == 0
    mine = jnp.where(first, mine, mine * gates_ref[...]).astype(BF16)
    for q in range(out_ref.shape[0]):
        out_ref[q] = mine


def send_slots(place_ref, gates_ref, blocks_ref, out_ref):
    total = blocks_ref[0].astype(F32)
    for q in range(1, blocks_ref.shape[0]):
        total = total + blocks_ref[q].astype(F32)
    total = total.astype(BF16).astype(F32)
    first = lax.axis_index("core") == 0
    total = jnp.where(first, total, total * gates_ref[...]).astype(BF16)
    to_messages(dot(place_ref[...], total, ((0,), (0,))), out_ref)


def receive_slots(pick_ref, arrived_ref, out_ref):
    rows = from_messages(arrived_ref, out_ref.shape[1] // LANES)
    out_ref[...] = dot(pick_ref[...], rows, ((1,), (0,))).astype(BF16)


def on_device(tokens, cotangent, slot_token, slot_gate, w_gate, w_up, w_down):
    w_gate, w_up, w_down = w_gate[0], w_up[0], w_down[0]
    n_ff = w_gate.shape[1]
    n_own, width = tokens.shape
    n_slots = slot_token.size
    core = lax.axis_index("core")
    first = core == 0
    n_chips = lax.axis_size(CHIPS)
    per_chip = n_slots // n_chips
    blocks = (n_chips, SEGMENTS, LANES)

    slots = slot_token.reshape(1, -1)
    ids = jnp.concatenate([slots // ID_BASE, slots % ID_BASE], axis=0).astype(BF16)
    ids = jnp.pad(ids, ((0, n_own - 2), (0, 2 * width - n_slots)))
    pairs = from_cores(jnp.concatenate([jnp.concatenate([tokens, cotangent], axis=1), ids], axis=0))
    sent, pick = on_vmem(
        functools.partial(send_tokens, n_slots),
        ((blocks, F32), ((2 * n_own, n_chips), BF16)),
        pairs,
    )
    arrived = lax.all_to_all(sent, CHIPS, 0, 0, tiled=True)
    place, my_gates = on_vmem(
        functools.partial(find_slots, 2 * n_own),
        (((per_chip, n_chips), BF16), ((per_chip, 1), F32)),
        slots,
        slot_gate.reshape(1, -1),
    )
    down = w_down.T
    blank = jnp.zeros_like(down)
    gate_up = jnp.concatenate([w_gate, w_up], axis=1)
    theirs = jnp.where(first, jnp.concatenate([down, blank], axis=1), gate_up)
    theirs = lax.ppermute(theirs, "core", [(0, 1), (1, 0)])
    weights = jnp.where(
        first,
        jnp.concatenate([gate_up, theirs], axis=1),
        jnp.concatenate([theirs[:, :n_ff], down, blank, blank], axis=1),
    )
    (copies,) = on_vmem(receive_tokens, (((n_chips, per_chip, width), BF16),), place, my_gates, arrived)
    rows = lax.all_to_all(copies, CHIPS, 0, 0, tiled=True).reshape(n_slots, width)
    weights, rows = lax.optimization_barrier((weights, rows))

    parts = dot(rows, weights, ((1,), (0,))).astype(BF16)
    sums = jnp.sum(exchange(parts, SHARD).astype(F32), axis=0)
    sums = from_cores(sums)
    trios = []
    for k in range(2):
        gate_pre = sums[0, :, 2 * k * n_ff : (2 * k + 1) * n_ff]
        up_pre = sums[0, :, (2 * k + 1) * n_ff : (2 * k + 2) * n_ff]
        grad_hidden = sums[1, :, k * n_ff : (k + 1) * n_ff]
        s = jax.nn.sigmoid(gate_pre)
        trios.append(
            (
                (gate_pre * s * up_pre).astype(BF16),
                (grad_hidden * up_pre * s * (1.0 + gate_pre * (1.0 - s))).astype(BF16),
                (grad_hidden * gate_pre * s).astype(BF16),
            )
        )
    (h0, g0, u0), (h1, g1, u1) = trios
    factors = jnp.concatenate([jnp.where(first, g0, h0), jnp.where(first, u0, h1), g1, u1], axis=1)
    factors = spread(factors, SHARD)

    total = dot(factors, weights, ((1,), (1,))).astype(BF16)
    total, rows, factors = lax.optimization_barrier((total, rows, factors))
    summands = exchange(total, CHIPS)
    other = lax.ppermute(jnp.concatenate([rows, factors[:, :n_ff]], axis=1), "core", [(0, 1), (1, 0)])
    factors, rows, other, summands = lax.optimization_barrier((factors, rows, other, summands))
    (back,) = on_vmem(send_slots, ((blocks, F32),), place, my_gates, summands)
    returned = lax.all_to_all(back, CHIPS, 0, 0, tiled=True)
    (chip_out,) = on_vmem(receive_slots, (((2 * n_own, width), BF16),), pick, returned)
    done = from_cores(chip_out)
    grad_tokens = lax.dynamic_slice_in_dim(done[0], core * n_own, n_own, 0)
    mixed = lax.dynamic_slice_in_dim(done[1], core * n_own, n_own, 0)

    inputs = jnp.where(first, rows, other[:, :width])
    scaled = jnp.where(first, other[:, :width], rows)
    hidden = jnp.where(first, other[:, width:], factors[:, n_ff : 2 * n_ff])
    grad_pre = lax.dynamic_slice_in_dim(factors, core * 2 * n_ff, 2 * n_ff, 1)
    grad_down = dot(hidden, scaled, ((0,), (0,))).astype(BF16)
    grad_gate = dot(inputs, grad_pre[:, :n_ff], ((0,), (0,))).astype(BF16)
    grad_up = dot(inputs, grad_pre[:, n_ff:], ((0,), (0,))).astype(BF16)
    return (mixed, grad_tokens, grad_gate[None], grad_up[None], grad_down[None])


def solution(mesh):
    fine = Mesh(mesh.devices.reshape(tuple(SIZES.values())), tuple(SIZES))
    return jax.shard_map(
        on_device,
        mesh=fine,
        in_specs=(
            P(DP, SHARD),
            P(DP, SHARD),
            P(),
            P(),
            P(None, SHARD, DP),
            P(None, SHARD, DP),
            P(None, DP, SHARD),
        ),
        out_specs=(
            P(DP, SHARD),
            P(DP, SHARD),
            P(None, SHARD, DP),
            P(None, SHARD, DP),
            P(None, DP, SHARD),
        ),
        check_vma=False,
    )
```

```python
import functools

import jax
import jax.numpy as jnp
from jax import lax
from jax.experimental import pallas as pl
from jax.experimental.pallas import tpu as pltpu
from jax.sharding import Mesh
from jax.sharding import PartitionSpec as P


BF16 = jnp.bfloat16
F32 = jnp.float32
CHIPS = ("z", "yh")
SHARD = ("yl", "x")
DP = ("z", "yh", "core")
SIZES = {"z": 8, "yh": 4, "core": 2, "yl": 2, "x": 4}


def exchange(rows, axes):
    n = lax.axis_size(axes)
    blocks = rows.reshape(n, rows.shape[0] // n, rows.shape[1])
    return lax.all_to_all(blocks, axes, 0, 0, tiled=True)


def spread(rows, axes):
    n = lax.axis_size(axes)
    blocks = jnp.broadcast_to(rows[None], (n, *rows.shape))
    out = lax.all_to_all(blocks, axes, 0, 0, tiled=True)
    return out.reshape(n * rows.shape[0], rows.shape[1])


def from_cores(rows):
    return lax.all_gather(rows, "core", axis=0, tiled=False)


def dot(a, b, dims):
    return lax.dot_general(a, b, (dims, ((), ())), preferred_element_type=F32)


def on_vmem(kernel, outs, *operands):
    vmem = pl.BlockSpec(memory_space=pltpu.VMEM)
    return pl.pallas_call(
        kernel,
        out_shape=tuple(jax.ShapeDtypeStruct(*o) for o in outs),
        in_specs=[vmem] * len(operands),
        out_specs=(vmem,) * len(outs),
        compiler_params=pltpu.CompilerParams(vmem_limit_bytes=4 << 20),
    )(*operands)


LANES = 128
SEGMENTS = 8


def to_messages(rows, out_ref):
    used = rows.shape[1] // LANES
    for k in range(used):
        out_ref[:, k, :] = rows[:, k * LANES : (k + 1) * LANES]
    if used < SEGMENTS:
        out_ref[:, used:, :] = jnp.zeros((rows.shape[0], SEGMENTS - used, LANES), F32)


def from_messages(ref, used):
    return jnp.concatenate([ref[:, k, :] for k in range(used)], axis=1).astype(BF16)


def send_tokens(slots_ref, pairs_ref, out_ref, pick_ref):
    n_tok, n_chips = pick_ref.shape
    n_own = n_tok // 2
    width = pairs_ref.shape[2] // 2
    chip = lax.axis_index("z") * lax.axis_size("yh") + lax.axis_index("yh")
    slots = slots_ref[...].astype(F32)
    n_slots = slots.shape[1]

    ids = (chip * n_tok + lax.broadcasted_iota(jnp.int32, (n_tok, n_slots), 0)).astype(F32)
    row = jnp.broadcast_to(slots, (n_tok, n_slots))
    rank = jnp.sum(jnp.where(row < ids, 1.0, 0.0), axis=1, keepdims=True).astype(jnp.int32)
    held = jnp.sum(jnp.where(row == ids, 1.0, 0.0), axis=1, keepdims=True)
    peer = lax.broadcasted_iota(jnp.int32, (n_tok, n_chips), 1)
    lane = jnp.where(held > 0.0, lax.rem(rank, n_chips), -1)
    pick_ref[...] = jnp.where(peer == lane, 1.0, 0.0).astype(BF16)

    first = lax.axis_index("core") == 0
    here = [
        jnp.where(first, pairs_ref[c, :n_own, :width].astype(F32), pairs_ref[c, :n_own, width:].astype(F32))
        for c in range(2)
    ]
    rows = jnp.concatenate(here, axis=0).astype(BF16)
    to_messages(dot(pick_ref[...], rows, ((0,), (0,))), out_ref)


def find_slots(n_tok, slots_ref, gates_ref, place_ref, my_gates_ref):
    per_chip, n_chips = place_ref.shape
    n_slots = slots_ref.shape[1]
    chip = lax.axis_index("z") * lax.axis_size("yh") + lax.axis_index("yh")
    slots = slots_ref[...]
    wide = jnp.broadcast_to(slots.astype(F32), (LANES, n_slots))
    column = jnp.transpose(wide)[:, :1]
    below = jnp.where(column < slots.astype(F32), 1.0, 0.0)
    ranks = jnp.sum(below, axis=0, keepdims=True).astype(jnp.int32)
    mine = chip + n_chips * lax.broadcasted_iota(jnp.int32, (per_chip, n_slots), 0)
    match = jnp.broadcast_to(ranks, (per_chip, n_slots)) == mine
    token = jnp.sum(jnp.where(match, slots.astype(F32), 0.0), axis=1, keepdims=True).astype(jnp.int32)
    my_gates_ref[...] = jnp.sum(jnp.where(match, gates_ref[...], 0.0), axis=1, keepdims=True)
    source = lax.broadcasted_iota(jnp.int32, (per_chip, n_chips), 1)
    place_ref[...] = jnp.where(lax.div(token, n_tok) == source, 1.0, 0.0).astype(BF16)


def receive_tokens(place_ref, gates_ref, arrived_ref, out_ref):
    rows = from_messages(arrived_ref, out_ref.shape[2] // LANES)
    mine = dot(place_ref[...], rows, ((1,), (0,)))
    first = lax.axis_index("core") == 0
    mine = jnp.where(first, mine, mine * gates_ref[...]).astype(BF16)
    for q in range(out_ref.shape[0]):
        out_ref[q] = mine


def send_slots(place_ref, gates_ref, blocks_ref, out_ref):
    total = blocks_ref[0].astype(F32)
    for q in range(1, blocks_ref.shape[0]):
        total = total + blocks_ref[q].astype(F32)
    total = total.astype(BF16).astype(F32)
    first = lax.axis_index("core") == 0
    total = jnp.where(first, total, total * gates_ref[...]).astype(BF16)
    to_messages(dot(place_ref[...], total, ((0,), (0,))), out_ref)


def receive_slots(pick_ref, arrived_ref, out_ref):
    rows = from_messages(arrived_ref, out_ref.shape[1] // LANES)
    out_ref[...] = dot(pick_ref[...], rows, ((1,), (0,))).astype(BF16)


def on_device(tokens, cotangent, slot_token, slot_gate, w_gate, w_up, w_down):
    w_gate, w_up, w_down = w_gate[0], w_up[0], w_down[0]
    n_ff = w_gate.shape[1]
    n_own, width = tokens.shape
    n_slots = slot_token.size
    core = lax.axis_index("core")
    first = core == 0
    n_chips = lax.axis_size(CHIPS)
    per_chip = n_slots // n_chips
    blocks = (n_chips, SEGMENTS, LANES)

    slots = slot_token.reshape(1, -1)
    pairs = from_cores(jnp.concatenate([tokens, cotangent], axis=1))
    sent, pick = on_vmem(send_tokens, ((blocks, F32), ((2 * n_own, n_chips), BF16)), slots, pairs)
    arrived = lax.all_to_all(sent, CHIPS, 0, 0, tiled=True)
    place, my_gates = on_vmem(
        functools.partial(find_slots, 2 * n_own),
        (((per_chip, n_chips), BF16), ((per_chip, 1), F32)),
        slots,
        slot_gate.reshape(1, -1),
    )
    down = w_down.T
    blank = jnp.zeros_like(down)
    gate_up = jnp.concatenate([w_gate, w_up], axis=1)
    theirs = jnp.where(first, jnp.concatenate([down, blank], axis=1), gate_up)
    theirs = lax.ppermute(theirs, "core", [(0, 1), (1, 0)])
    weights = jnp.where(
        first,
        jnp.concatenate([gate_up, theirs], axis=1),
        jnp.concatenate([theirs[:, :n_ff], down, blank, blank], axis=1),
    )
    (copies,) = on_vmem(receive_tokens, (((n_chips, per_chip, width), BF16),), place, my_gates, arrived)
    rows = lax.all_to_all(copies, CHIPS, 0, 0, tiled=True)
    rows = rows.reshape(n_slots, width)
    weights, rows = lax.optimization_barrier((weights, rows))

    parts = dot(rows, weights, ((1,), (0,))).astype(BF16)
    sums = jnp.sum(exchange(parts, SHARD).astype(F32), axis=0)
    sums = from_cores(sums)
    trios = []
    for k in range(2):
        gate_pre = sums[0, :, 2 * k * n_ff : (2 * k + 1) * n_ff]
        up_pre = sums[0, :, (2 * k + 1) * n_ff : (2 * k + 2) * n_ff]
        grad_hidden = sums[1, :, k * n_ff : (k + 1) * n_ff]
        s = jax.nn.sigmoid(gate_pre)
        trios.append(
            (
                (gate_pre * s * up_pre).astype(BF16),
                (grad_hidden * up_pre * s * (1.0 + gate_pre * (1.0 - s))).astype(BF16),
                (grad_hidden * gate_pre * s).astype(BF16),
            )
        )
    (h0, g0, u0), (h1, g1, u1) = trios
    factors = jnp.concatenate([jnp.where(first, g0, h0), jnp.where(first, u0, h1), g1, u1], axis=1)
    factors = spread(factors, SHARD)

    total = dot(factors, weights, ((1,), (1,))).astype(BF16)
    total, rows, factors = lax.optimization_barrier((total, rows, factors))
    summands = exchange(total, CHIPS)
    other = lax.ppermute(jnp.concatenate([rows, factors[:, :n_ff]], axis=1), "core", [(0, 1), (1, 0)])
    factors, rows, other = lax.optimization_barrier((factors, rows, other))
    (back,) = on_vmem(send_slots, ((blocks, F32),), place, my_gates, summands)
    returned = lax.all_to_all(back, CHIPS, 0, 0, tiled=True)
    (chip_out,) = on_vmem(receive_slots, (((2 * n_own, width), BF16),), pick, returned)
    done = from_cores(chip_out)
    grad_tokens = lax.dynamic_slice_in_dim(done[0], core * n_own, n_own, 0)
    mixed = lax.dynamic_slice_in_dim(done[1], core * n_own, n_own, 0)

    inputs = jnp.where(first, rows, other[:, :width])
    scaled = jnp.where(first, other[:, :width], rows)
    hidden = jnp.where(first, other[:, width:], factors[:, n_ff : 2 * n_ff])
    grad_pre = lax.dynamic_slice_in_dim(factors, core * 2 * n_ff, 2 * n_ff, 1)
    grad_down = dot(hidden, scaled, ((0,), (0,))).astype(BF16)
    grad_gate = dot(inputs, grad_pre[:, :n_ff], ((0,), (0,))).astype(BF16)
    grad_up = dot(inputs, grad_pre[:, n_ff:], ((0,), (0,))).astype(BF16)
    return (mixed, grad_tokens, grad_gate[None], grad_up[None], grad_down[None])


def solution(mesh):
    fine = Mesh(mesh.devices.reshape(tuple(SIZES.values())), tuple(SIZES))
    return jax.shard_map(
        on_device,
        mesh=fine,
        in_specs=(
            P(DP, SHARD),
            P(DP, SHARD),
            P(),
            P(),
            P(None, SHARD, DP),
            P(None, SHARD, DP),
            P(None, DP, SHARD),
        ),
        out_specs=(
            P(DP, SHARD),
            P(DP, SHARD),
            P(None, SHARD, DP),
            P(None, SHARD, DP),
            P(None, DP, SHARD),
        ),
        check_vma=False,
    )
```

```python
import functools

import jax
import jax.numpy as jnp
from jax import lax
from jax.experimental import pallas as pl
from jax.experimental.pallas import tpu as pltpu
from jax.sharding import Mesh
from jax.sharding import PartitionSpec as P


BF16 = jnp.bfloat16
F32 = jnp.float32
CHIPS = ("z", "yh")
SHARD = ("yl", "x")
DP = ("z", "yh", "core")
SIZES = {"z": 8, "yh": 4, "core": 2, "yl": 2, "x": 4}


def exchange(rows, axes):
    n = lax.axis_size(axes)
    blocks = rows.reshape(n, rows.shape[0] // n, rows.shape[1])
    return lax.all_to_all(blocks, axes, 0, 0, tiled=True)


def spread(rows, axes):
    n = lax.axis_size(axes)
    blocks = jnp.broadcast_to(rows[None], (n, *rows.shape))
    out = lax.all_to_all(blocks, axes, 0, 0, tiled=True)
    return out.reshape(n * rows.shape[0], rows.shape[1])


def from_cores(rows):
    return lax.all_gather(rows, "core", axis=0, tiled=False)


def dot(a, b, dims):
    return lax.dot_general(a, b, (dims, ((), ())), preferred_element_type=F32)


def on_vmem(kernel, outs, *operands):
    vmem = pl.BlockSpec(memory_space=pltpu.VMEM)
    return pl.pallas_call(
        kernel,
        out_shape=tuple(jax.ShapeDtypeStruct(*o) for o in outs),
        in_specs=[vmem] * len(operands),
        out_specs=(vmem,) * len(outs),
        compiler_params=pltpu.CompilerParams(vmem_limit_bytes=4 << 20),
    )(*operands)


LANES = 128
SEGMENTS = 8


def to_messages(rows, out_ref):
    used = rows.shape[1] // LANES
    for k in range(used):
        out_ref[:, k, :] = rows[:, k * LANES : (k + 1) * LANES]
    if used < SEGMENTS:
        out_ref[:, used:, :] = jnp.zeros((rows.shape[0], SEGMENTS - used, LANES), F32)


def from_messages(ref, used):
    return jnp.concatenate([ref[:, k, :] for k in range(used)], axis=1).astype(BF16)


def send_tokens(slots_ref, pairs_ref, out_ref, pick_ref):
    n_tok, n_chips = pick_ref.shape
    n_own = n_tok // 2
    width = pairs_ref.shape[2] // 2
    chip = lax.axis_index("z") * lax.axis_size("yh") + lax.axis_index("yh")
    slots = slots_ref[...].astype(F32)
    n_slots = slots.shape[1]

    ids = (chip * n_tok + lax.broadcasted_iota(jnp.int32, (n_tok, n_slots), 0)).astype(F32)
    row = jnp.broadcast_to(slots, (n_tok, n_slots))
    rank = jnp.sum(jnp.where(row < ids, 1.0, 0.0), axis=1, keepdims=True).astype(jnp.int32)
    held = jnp.sum(jnp.where(row == ids, 1.0, 0.0), axis=1, keepdims=True)
    peer = lax.broadcasted_iota(jnp.int32, (n_tok, n_chips), 1)
    lane = jnp.where(held > 0.0, lax.rem(rank, n_chips), -1)
    pick_ref[...] = jnp.where(peer == lane, 1.0, 0.0).astype(BF16)

    first = lax.axis_index("core") == 0
    here = [
        jnp.where(first, pairs_ref[c, :n_own, :width].astype(F32), pairs_ref[c, :n_own, width:].astype(F32))
        for c in range(2)
    ]
    rows = jnp.concatenate(here, axis=0).astype(BF16)
    to_messages(dot(pick_ref[...], rows, ((0,), (0,))), out_ref)


def find_slots(n_tok, slots_ref, gates_ref, place_ref, back_ref, fetch_ref, my_gates_ref):
    per_chip, n_chips = place_ref.shape
    n_slots = slots_ref.shape[1]
    chip = lax.axis_index("z") * lax.axis_size("yh") + lax.axis_index("yh")
    slots = slots_ref[...]
    wide = jnp.broadcast_to(slots.astype(F32), (LANES, n_slots))
    column = jnp.transpose(wide)[:, :1]
    below = jnp.where(column < slots.astype(F32), 1.0, 0.0)
    ranks = jnp.sum(below, axis=0, keepdims=True).astype(jnp.int32)
    mine = chip + n_chips * lax.broadcasted_iota(jnp.int32, (per_chip, n_slots), 0)
    match = jnp.broadcast_to(ranks, (per_chip, n_slots)) == mine
    token = jnp.sum(jnp.where(match, slots.astype(F32), 0.0), axis=1, keepdims=True).astype(jnp.int32)
    my_gates_ref[...] = jnp.sum(jnp.where(match, gates_ref[...], 0.0), axis=1, keepdims=True)
    source = lax.broadcasted_iota(jnp.int32, (per_chip, n_chips), 1)
    place_ref[...] = jnp.where(lax.div(token, n_tok) == source, 1.0, 0.0).astype(BF16)

    n_own, n_dev = n_tok // 2, back_ref.shape[1]
    device = lax.broadcasted_iota(jnp.int32, (per_chip, n_dev), 1)
    back_ref[...] = jnp.where(lax.div(token, n_own) == device, 1.0, 0.0).astype(BF16)
    line = lax.broadcasted_iota(jnp.int32, (n_tok, n_slots), 0)
    ids = (2 * chip + lax.axis_index("core")) * n_own + lax.rem(line, n_own)
    row = jnp.broadcast_to(slots, (n_tok, n_slots))
    rank = jnp.sum(jnp.where(row < ids, 1.0, 0.0), axis=1, keepdims=True).astype(jnp.int32)
    held = jnp.sum(jnp.where(row == ids, 1.0, 0.0), axis=1, keepdims=True)
    role = lax.div(lax.broadcasted_iota(jnp.int32, (n_tok, n_dev), 0), n_own)
    peer = lax.broadcasted_iota(jnp.int32, (n_tok, n_dev), 1)
    lane = jnp.where(held > 0.0, 2 * lax.rem(rank, n_chips), -2) + role
    fetch_ref[...] = jnp.where((peer == lane) & (held > 0.0), 1.0, 0.0).astype(BF16)


def receive_tokens(place_ref, gates_ref, arrived_ref, out_ref):
    rows = from_messages(arrived_ref, out_ref.shape[2] // LANES)
    mine = dot(place_ref[...], rows, ((1,), (0,)))
    first = lax.axis_index("core") == 0
    mine = jnp.where(first, mine, mine * gates_ref[...]).astype(BF16)
    for q in range(out_ref.shape[0]):
        out_ref[q] = mine


def send_slots(place_ref, gates_ref, blocks_ref, out_ref):
    total = blocks_ref[0].astype(F32)
    for q in range(1, blocks_ref.shape[0]):
        total = total + blocks_ref[q].astype(F32)
    total = total.astype(BF16).astype(F32)
    first = lax.axis_index("core") == 0
    total = jnp.where(first, total, total * gates_ref[...]).astype(BF16)
    to_messages(dot(place_ref[...], total, ((0,), (0,))), out_ref)


def receive_slots(fetch_ref, arrived_ref, grad_ref, mixed_ref):
    n_own = grad_ref.shape[0]
    rows = from_messages(arrived_ref, grad_ref.shape[1] // LANES)
    found = dot(fetch_ref[...], rows, ((1,), (0,))).astype(BF16)
    grad_ref[...] = found[:n_own]
    mixed_ref[...] = found[n_own:]


def on_device(tokens, cotangent, slot_token, slot_gate, w_gate, w_up, w_down):
    w_gate, w_up, w_down = w_gate[0], w_up[0], w_down[0]
    n_ff = w_gate.shape[1]
    n_own, width = tokens.shape
    n_slots = slot_token.size
    core = lax.axis_index("core")
    first = core == 0
    n_chips = lax.axis_size(CHIPS)
    per_chip = n_slots // n_chips
    blocks = (n_chips, SEGMENTS, LANES)

    slots = slot_token.reshape(1, -1)
    pairs = from_cores(jnp.concatenate([tokens, cotangent], axis=1))
    sent, _ = on_vmem(send_tokens, ((blocks, F32), ((2 * n_own, n_chips), BF16)), slots, pairs)
    arrived = lax.all_to_all(sent, CHIPS, 0, 0, tiled=True)
    place, to_owner, fetch, my_gates = on_vmem(
        functools.partial(find_slots, 2 * n_own),
        (
            ((per_chip, n_chips), BF16),
            ((per_chip, 2 * n_chips), BF16),
            ((2 * n_own, 2 * n_chips), BF16),
            ((per_chip, 1), F32),
        ),
        slots,
        slot_gate.reshape(1, -1),
    )
    down = w_down.T
    blank = jnp.zeros_like(down)
    gate_up = jnp.concatenate([w_gate, w_up], axis=1)
    theirs = jnp.where(first, jnp.concatenate([down, blank], axis=1), gate_up)
    theirs = lax.ppermute(theirs, "core", [(0, 1), (1, 0)])
    weights = jnp.where(
        first,
        jnp.concatenate([gate_up, theirs], axis=1),
        jnp.concatenate([theirs[:, :n_ff], down, blank, blank], axis=1),
    )
    (copies,) = on_vmem(receive_tokens, (((n_chips, per_chip, width), BF16),), place, my_gates, arrived)
    rows = lax.all_to_all(copies, CHIPS, 0, 0, tiled=True)
    rows = rows.reshape(n_slots, width)
    weights, rows = lax.optimization_barrier((weights, rows))

    parts = dot(rows, weights, ((1,), (0,))).astype(BF16)
    sums = jnp.sum(exchange(parts, SHARD).astype(F32), axis=0)
    sums = from_cores(sums)
    trios = []
    for k in range(2):
        gate_pre = sums[0, :, 2 * k * n_ff : (2 * k + 1) * n_ff]
        up_pre = sums[0, :, (2 * k + 1) * n_ff : (2 * k + 2) * n_ff]
        grad_hidden = sums[1, :, k * n_ff : (k + 1) * n_ff]
        s = jax.nn.sigmoid(gate_pre)
        trios.append(
            (
                (gate_pre * s * up_pre).astype(BF16),
                (grad_hidden * up_pre * s * (1.0 + gate_pre * (1.0 - s))).astype(BF16),
                (grad_hidden * gate_pre * s).astype(BF16),
            )
        )
    (h0, g0, u0), (h1, g1, u1) = trios
    factors = jnp.concatenate([jnp.where(first, g0, h0), jnp.where(first, u0, h1), g1, u1], axis=1)
    factors = spread(factors, SHARD)

    total = dot(factors, weights, ((1,), (1,))).astype(BF16)
    total, rows, factors = lax.optimization_barrier((total, rows, factors))
    summands = exchange(total, CHIPS)
    other = lax.ppermute(jnp.concatenate([rows, factors[:, :n_ff]], axis=1), "core", [(0, 1), (1, 0)])
    factors, rows, other = lax.optimization_barrier((factors, rows, other))
    messages = (2 * n_chips, SEGMENTS, LANES)
    (back,) = on_vmem(send_slots, ((messages, F32),), to_owner, my_gates, summands)
    returned = lax.all_to_all(back.astype(BF16), DP, 0, 0, tiled=True).astype(F32)
    grad_tokens, mixed = on_vmem(receive_slots, (((n_own, width), BF16),) * 2, fetch, returned)

    inputs = jnp.where(first, rows, other[:, :width])
    scaled = jnp.where(first, other[:, :width], rows)
    hidden = jnp.where(first, other[:, width:], factors[:, n_ff : 2 * n_ff])
    grad_pre = jnp.where(first, factors[:, : 2 * n_ff], factors[:, 2 * n_ff :])
    grad_down = dot(hidden, scaled, ((0,), (0,))).astype(BF16)
    grad_gate = dot(inputs, grad_pre[:, :n_ff], ((0,), (0,))).astype(BF16)
    grad_up = dot(inputs, grad_pre[:, n_ff:], ((0,), (0,))).astype(BF16)
    return (mixed, grad_tokens, grad_gate[None], grad_up[None], grad_down[None])


def solution(mesh):
    fine = Mesh(mesh.devices.reshape(tuple(SIZES.values())), tuple(SIZES))
    return jax.shard_map(
        on_device,
        mesh=fine,
        in_specs=(
            P(DP, SHARD),
            P(DP, SHARD),
            P(),
            P(),
            P(None, SHARD, DP),
            P(None, SHARD, DP),
            P(None, DP, SHARD),
        ),
        out_specs=(
            P(DP, SHARD),
            P(DP, SHARD),
            P(None, SHARD, DP),
            P(None, SHARD, DP),
            P(None, DP, SHARD),
        ),
        check_vma=False,
    )
```

```python
import functools

import jax
import jax.numpy as jnp
from jax import lax
from jax.experimental import pallas as pl
from jax.experimental.pallas import tpu as pltpu
from jax.sharding import Mesh
from jax.sharding import PartitionSpec as P


BF16 = jnp.bfloat16
F32 = jnp.float32
CHIPS = ("z", "yh")
SHARD = ("yl", "x")
DP = ("z", "yh", "core")
SIZES = {"z": 8, "yh": 4, "core": 2, "yl": 2, "x": 4}


def exchange(rows, axes):
    n = lax.axis_size(axes)
    blocks = rows.reshape(n, rows.shape[0] // n, rows.shape[1])
    return lax.all_to_all(blocks, axes, 0, 0, tiled=True)


def spread(rows, axes):
    n = lax.axis_size(axes)
    blocks = jnp.broadcast_to(rows[None], (n, *rows.shape))
    out = lax.all_to_all(blocks, axes, 0, 0, tiled=True)
    return out.reshape(n * rows.shape[0], rows.shape[1])


def from_cores(rows):
    return lax.all_gather(rows, "core", axis=0, tiled=False)


def dot(a, b, dims):
    return lax.dot_general(a, b, (dims, ((), ())), preferred_element_type=F32)


def on_vmem(kernel, outs, *operands):
    vmem = pl.BlockSpec(memory_space=pltpu.VMEM)
    return pl.pallas_call(
        kernel,
        out_shape=tuple(jax.ShapeDtypeStruct(*o) for o in outs),
        in_specs=[vmem] * len(operands),
        out_specs=(vmem,) * len(outs),
        compiler_params=pltpu.CompilerParams(vmem_limit_bytes=4 << 20),
    )(*operands)


LANES = 128
SEGMENTS = 8


def to_messages(rows, out_ref):
    used = rows.shape[1] // LANES
    for k in range(used):
        out_ref[:, k, :] = rows[:, k * LANES : (k + 1) * LANES]
    if used < SEGMENTS:
        out_ref[:, used:, :] = jnp.zeros((rows.shape[0], SEGMENTS - used, LANES), F32)


def from_messages(ref, used):
    return jnp.concatenate([ref[:, k, :] for k in range(used)], axis=1).astype(BF16)


def send_tokens(slots_ref, pairs_ref, out_ref, pick_ref):
    n_tok, n_chips = pick_ref.shape
    n_own = n_tok // 2
    width = pairs_ref.shape[2] // 2
    chip = lax.axis_index("z") * lax.axis_size("yh") + lax.axis_index("yh")
    slots = slots_ref[...].astype(F32)
    n_slots = slots.shape[1]

    ids = (chip * n_tok + lax.broadcasted_iota(jnp.int32, (n_tok, n_slots), 0)).astype(F32)
    row = jnp.broadcast_to(slots, (n_tok, n_slots))
    rank = jnp.sum(jnp.where(row < ids, 1.0, 0.0), axis=1, keepdims=True).astype(jnp.int32)
    held = jnp.sum(jnp.where(row == ids, 1.0, 0.0), axis=1, keepdims=True)
    peer = lax.broadcasted_iota(jnp.int32, (n_tok, n_chips), 1)
    lane = jnp.where(held > 0.0, lax.rem(rank, n_chips), -1)
    pick_ref[...] = jnp.where(peer == lane, 1.0, 0.0).astype(BF16)

    first = lax.axis_index("core") == 0
    here = [
        jnp.where(first, pairs_ref[c, :n_own, :width].astype(F32), pairs_ref[c, :n_own, width:].astype(F32))
        for c in range(2)
    ]
    rows = jnp.concatenate(here, axis=0).astype(BF16)
    to_messages(dot(pick_ref[...], rows, ((0,), (0,))), out_ref)


def find_slots(n_tok, slots_ref, gates_ref, place_ref, my_gates_ref):
    per_chip, n_chips = place_ref.shape
    n_slots = slots_ref.shape[1]
    chip = lax.axis_index("z") * lax.axis_size("yh") + lax.axis_index("yh")
    slots = slots_ref[...]
    wide = jnp.broadcast_to(slots.astype(F32), (LANES, n_slots))
    column = jnp.transpose(wide)[:, :1]
    below = jnp.where(column < slots.astype(F32), 1.0, 0.0)
    ranks = jnp.sum(below, axis=0, keepdims=True).astype(jnp.int32)
    mine = chip + n_chips * lax.broadcasted_iota(jnp.int32, (per_chip, n_slots), 0)
    match = jnp.broadcast_to(ranks, (per_chip, n_slots)) == mine
    token = jnp.sum(jnp.where(match, slots.astype(F32), 0.0), axis=1, keepdims=True).astype(jnp.int32)
    my_gates_ref[...] = jnp.sum(jnp.where(match, gates_ref[...], 0.0), axis=1, keepdims=True)
    source = lax.broadcasted_iota(jnp.int32, (per_chip, n_chips), 1)
    place_ref[...] = jnp.where(lax.div(token, n_tok) == source, 1.0, 0.0).astype(BF16)


def receive_tokens(place_ref, gates_ref, arrived_ref, out_ref):
    rows = from_messages(arrived_ref, out_ref.shape[2] // LANES)
    mine = dot(place_ref[...], rows, ((1,), (0,)))
    first = lax.axis_index("core") == 0
    mine = jnp.where(first, mine, mine * gates_ref[...]).astype(BF16)
    for q in range(out_ref.shape[0]):
        out_ref[q] = mine


def send_slots(place_ref, gates_ref, blocks_ref, out_ref):
    total = blocks_ref[0].astype(F32)
    for q in range(1, blocks_ref.shape[0]):
        total = total + blocks_ref[q].astype(F32)
    total = total.astype(BF16).astype(F32)
    first = lax.axis_index("core") == 0
    total = jnp.where(first, total, total * gates_ref[...]).astype(BF16)
    to_messages(dot(place_ref[...], total, ((0,), (0,))), out_ref)


def receive_slots(pick_ref, arrived_ref, out_ref):
    rows = from_messages(arrived_ref, out_ref.shape[1] // LANES)
    out_ref[...] = dot(pick_ref[...], rows, ((1,), (0,))).astype(BF16)


def on_device(tokens, cotangent, slot_token, slot_gate, w_gate, w_up, w_down):
    w_gate, w_up, w_down = w_gate[0], w_up[0], w_down[0]
    n_ff = w_gate.shape[1]
    n_own, width = tokens.shape
    n_slots = slot_token.size
    core = lax.axis_index("core")
    first = core == 0
    n_chips = lax.axis_size(CHIPS)
    per_chip = n_slots // n_chips
    blocks = (n_chips, SEGMENTS, LANES)

    slots = slot_token.reshape(1, -1)
    pairs = from_cores(jnp.concatenate([tokens, cotangent], axis=1))
    sent, pick = on_vmem(send_tokens, ((blocks, F32), ((2 * n_own, n_chips), BF16)), slots, pairs)
    arrived = lax.all_to_all(sent, CHIPS, 0, 0, tiled=True)
    place, my_gates = on_vmem(
        functools.partial(find_slots, 2 * n_own),
        (((per_chip, n_chips), BF16), ((per_chip, 1), F32)),
        slots,
        slot_gate.reshape(1, -1),
    )
    down = w_down.T
    blank = jnp.zeros_like(down)
    gate_up = jnp.concatenate([w_gate, w_up], axis=1)
    theirs = jnp.where(first, jnp.concatenate([down, blank], axis=1), gate_up)
    theirs = lax.ppermute(theirs, "core", [(0, 1), (1, 0)])
    weights = jnp.where(
        first,
        jnp.concatenate([gate_up, theirs], axis=1),
        jnp.concatenate([theirs[:, :n_ff], down, blank, blank], axis=1),
    )
    (copies,) = on_vmem(receive_tokens, (((n_chips, per_chip, width), BF16),), place, my_gates, arrived)
    rows = lax.all_to_all(copies, CHIPS, 0, 0, tiled=True)
    rows = rows.reshape(n_slots, width)
    weights, rows = lax.optimization_barrier((weights, rows))

    parts = dot(rows, weights, ((1,), (0,))).astype(BF16)
    sums = jnp.sum(exchange(parts, SHARD).astype(F32), axis=0)
    sums = from_cores(sums)
    trios = []
    for k in range(2):
        gate_pre = sums[0, :, 2 * k * n_ff : (2 * k + 1) * n_ff]
        up_pre = sums[0, :, (2 * k + 1) * n_ff : (2 * k + 2) * n_ff]
        grad_hidden = sums[1, :, k * n_ff : (k + 1) * n_ff]
        s = jax.nn.sigmoid(gate_pre)
        trios.append(
            (
                (gate_pre * s * up_pre).astype(BF16),
                (grad_hidden * up_pre * s * (1.0 + gate_pre * (1.0 - s))).astype(BF16),
                (grad_hidden * gate_pre * s).astype(BF16),
            )
        )
    (h0, g0, u0), (h1, g1, u1) = trios
    factors = jnp.concatenate([jnp.where(first, g0, h0), jnp.where(first, u0, h1), g1, u1], axis=1)
    factors = spread(factors, SHARD)

    total = dot(factors, weights, ((1,), (1,))).astype(BF16)
    total, rows, factors = lax.optimization_barrier((total, rows, factors))
    summands = exchange(total, CHIPS)
    other = lax.ppermute(jnp.concatenate([rows, factors[:, :n_ff]], axis=1), "core", [(0, 1), (1, 0)])
    factors, rows, other = lax.optimization_barrier((factors, rows, other))
    (back,) = on_vmem(send_slots, ((blocks, F32),), place, my_gates, summands)
    returned = lax.all_to_all(back.astype(BF16), CHIPS, 0, 0, tiled=True).astype(F32)
    (chip_out,) = on_vmem(receive_slots, (((2 * n_own, width), BF16),), pick, returned)
    done = from_cores(chip_out)
    grad_tokens = jnp.where(first, done[0, :n_own], done[0, n_own:])
    mixed = jnp.where(first, done[1, :n_own], done[1, n_own:])

    inputs = jnp.where(first, rows, other[:, :width])
    scaled = jnp.where(first, other[:, :width], rows)
    hidden = jnp.where(first, other[:, width:], factors[:, n_ff : 2 * n_ff])
    grad_pre = jnp.where(first, factors[:, : 2 * n_ff], factors[:, 2 * n_ff :])
    grad_down = dot(hidden, scaled, ((0,), (0,))).astype(BF16)
    grad_gate = dot(inputs, grad_pre[:, :n_ff], ((0,), (0,))).astype(BF16)
    grad_up = dot(inputs, grad_pre[:, n_ff:], ((0,), (0,))).astype(BF16)
    return (mixed, grad_tokens, grad_gate[None], grad_up[None], grad_down[None])


def solution(mesh):
    fine = Mesh(mesh.devices.reshape(tuple(SIZES.values())), tuple(SIZES))
    return jax.shard_map(
        on_device,
        mesh=fine,
        in_specs=(
            P(DP, SHARD),
            P(DP, SHARD),
            P(),
            P(),
            P(None, SHARD, DP),
            P(None, SHARD, DP),
            P(None, DP, SHARD),
        ),
        out_specs=(
            P(DP, SHARD),
            P(DP, SHARD),
            P(None, SHARD, DP),
            P(None, SHARD, DP),
            P(None, DP, SHARD),
        ),
        check_vma=False,
    )
```
